256 devices in a mesh: replica: 4 (over y_hi, core), fsdp: 64 (over y_lo, x, z).
Axes of the slice: x: 4, y: 4 (y_hi: 2, y_lo: 2; y = y_hi * 2 + y_lo), z: 8, core: 2. Of those that a mesh axis runs over, the one named last changes fastest.
Arguments:
- layer_input: bfloat16 [2, 32768, 4096], P(None, ('replica', 'fsdp')), may hold values from -6 to 6
- queries: bfloat16 [2, 32768, 4096], P(None, ('replica', 'fsdp')), may hold values from -100 to 100
- keys: bfloat16 [2, 32768, 512], P(None, ('replica', 'fsdp')), may hold values from -8 to 8
- targets: bfloat16 [2, 32768, 4096], P(None, ('replica', 'fsdp')), may hold values from -6 to 6
- value_weight: float32 [4096, 512], P('fsdp'), may hold values from -6 to 6
- outer_momentum: float32 [4096, 512], P('fsdp'), may hold values from -0.6 to 0.6
Outputs:
- new_weight: float32 [4096, 512], P('fsdp')
- new_momentum: float32 [4096, 512], P('fsdp')
The draws below stay inside these ranges and needn't reach their ends.
All inputs are finite; a program needn't handle non-finite values.
Results may differ from the reference program's by a relative error of at most 0.0017.
Values may be sent and summed in bfloat16 or wider, within the bound.
No kernel may reach another device: no remote copies, remote signals or barrier semaphores. Data moves between devices by JAX's collectives and lax.ppermute only.
A program may use at most 64 MiB of HBM per device.

```python
import math
import jax
import jax.numpy as jnp
from jax import lax

D = 4096
QH = 32
KVH = 4
HD = 128
STEPS = 2
TOK_DEV = 128
TOKENS = 32768
N_REPLICA = 4
N_FSDP = 64


def attention_pair(seed_key):
    base = jax.random.fold_in(seed_key, 911)
    key_query, key_key = jax.random.split(base, 2)
    sequences = TOKENS // TOK_DEV
    group_size = QH // KVH
    key_rows = jax.random.normal(key_key, (STEPS, sequences, TOK_DEV, KVH, HD), jnp.float32)
    query_rows = jax.random.normal(key_query, (STEPS, sequences, TOK_DEV, KVH, group_size, HD), jnp.float32)
    query_rows = jnp.clip(query_rows, -100.0, 100.0).reshape(STEPS, TOKENS, QH * HD)
    key_rows = jnp.clip(key_rows, -8.0, 8.0).reshape(STEPS, TOKENS, KVH * HD)
    return (query_rows, key_rows)


def draw_queries(key, part):
    return attention_pair(key)[0].astype(jnp.bfloat16)


def draw_keys(key, part):
    return attention_pair(key)[1].astype(jnp.bfloat16)


def shard_levels(key, shape, cuts, least, high):
    loudness, own = 1.0, jax.random.fold_in(key, 6)
    for dim, blocks in cuts:
        heights = jnp.exp(jax.random.uniform(jax.random.fold_in(own, dim), (blocks,), jnp.float32, least / len(cuts), high / len(cuts)))
        loudness = loudness * jnp.repeat(heights, shape[dim] // blocks).reshape([-1 if axis == dim else 1 for axis in range(len(shape))])
    return loudness


def normal_values(stream_key, extent, spread, bound, shards=(), kind=jnp.bfloat16):
    result = spread * jax.random.normal(stream_key, extent, jnp.float32)
    if shards:
        result = result * shard_levels(stream_key, extent, shards, -0.22, 0.18)
    return jnp.clip(result, -bound, bound).astype(kind)


def setup_inputs(seed: int = 0) -> dict:
    arg_keys = jax.random.split(jax.random.key(seed), 7)
    return {
        "layer_input": normal_values(arg_keys[0], (STEPS, TOKENS, D), 1.0, 6.0, ((1, 256),)),
        "queries": draw_queries(jax.random.fold_in(arg_keys[6], 71), 0),
        "keys": draw_keys(jax.random.fold_in(arg_keys[6], 71), 0),
        "targets": normal_values(arg_keys[3], (STEPS, TOKENS, QH * HD), 1.0, 6.0, ((1, 256),)),
        "value_weight": normal_values(arg_keys[4], (D, KVH * HD), 1.0, 6.0, ((0, 64),), jnp.float32),
        "outer_momentum": normal_values(arg_keys[5], (D, KVH * HD), 0.1, 0.6, ((0, 64),), jnp.float32),
    }


beta_one = 0.9
beta_two = 0.95
inner_rate = 0.05
decay_rate = 0.1
outer_rate = 0.7
outer_mu = 0.9

def sequence_grad(query_rows, key_rows, values, target_rows):
    group_size = QH // KVH
    length = query_rows.shape[0]
    query_heads = query_rows.astype(jnp.float32).reshape(length, KVH, group_size, HD)
    key_heads = key_rows.astype(jnp.float32).reshape(length, KVH, HD)
    scores = jnp.einsum('qgjd,kgd->gjqk', query_heads, key_heads) / math.sqrt(HD)
    causal = jnp.arange(length)[:, None] >= jnp.arange(length)[None, :]
    scores = jnp.where(causal, scores, -1e+30)
    highest = lax.optimization_barrier(jnp.max(scores, axis=-1, keepdims=True))
    expd = jnp.exp(scores - highest)
    attention = (expd / lax.optimization_barrier(jnp.sum(expd, axis=-1, keepdims=True))).astype(jnp.bfloat16)
    attn_wide = attention.astype(jnp.float32)
    value_heads = values.astype(jnp.float32).reshape(length, KVH, HD)
    attended = jnp.einsum('gjqk,kgd->qgjd', attn_wide, value_heads).reshape(length, QH * HD)
    out_grad = ((attended - target_rows.astype(jnp.float32)) / (TOK_DEV * N_FSDP)).astype(jnp.bfloat16)
    grad_heads = out_grad.astype(jnp.float32).reshape(length, KVH, group_size, HD)
    value_grad = jnp.einsum('gjqk,qgjd->kgd', attn_wide, grad_heads).reshape(length, KVH * HD)
    return value_grad.astype(jnp.bfloat16)

def replica_round(value_weight, layer_input, queries, keys, targets, replica):
    tok_rep = TOK_DEV * N_FSDP
    adam_floor = math.sqrt(QH // KVH / (tok_rep * D))
    first_row = replica * tok_rep
    weights_now = value_weight
    moment_one = jnp.zeros_like(value_weight)
    moment_two = jnp.zeros_like(value_weight)
    for step_index in range(STEPS):
        inputs = layer_input[step_index, first_row:first_row + tok_rep]
        weights_bf = weights_now.astype(jnp.bfloat16)
        values = (jnp.dot(inputs, weights_bf, preferred_element_type=jnp.float32) / math.sqrt(D)).astype(jnp.bfloat16)
        query_seq = queries[step_index, first_row:first_row + tok_rep].reshape(N_FSDP, TOK_DEV, QH * HD)
        key_seq = keys[step_index, first_row:first_row + tok_rep].reshape(N_FSDP, TOK_DEV, KVH * HD)
        value_seq = values.reshape(N_FSDP, TOK_DEV, KVH * HD)
        target_seq = targets[step_index, first_row:first_row + tok_rep].reshape(N_FSDP, TOK_DEV, QH * HD)
        value_grad = lax.map(lambda group: sequence_grad(group[0], group[1], group[2], group[3]), (query_seq, key_seq, value_seq, target_seq))
        value_grad = value_grad.reshape(tok_rep, KVH * HD)
        gradient = jnp.dot(inputs.T, value_grad, preferred_element_type=jnp.float32) / math.sqrt(D)
        moment_one = beta_one * moment_one + (1.0 - beta_one) * gradient
        moment_two = beta_two * moment_two + (1.0 - beta_two) * gradient * gradient
        corrected_one = moment_one / (1.0 - beta_one ** (step_index + 1))
        corrected_two = moment_two / (1.0 - beta_two ** (step_index + 1))
        weights_now = weights_now - inner_rate * (corrected_one / (jnp.sqrt(corrected_two) + adam_floor) + decay_rate * weights_now)
    return weights_now

def reference(layer_input, queries, keys, targets, value_weight, outer_momentum):
    total_delta = jnp.zeros_like(value_weight)
    for replica in range(N_REPLICA):
        total_delta = total_delta + (value_weight - replica_round(value_weight, layer_input, queries, keys, targets, replica))
    mean_delta = total_delta / N_REPLICA
    new_momentum = outer_mu * outer_momentum + mean_delta
    new_weight = value_weight - outer_rate * (mean_delta + outer_mu * new_momentum)
    return (new_weight, new_momentum)
```

```python
import math

import jax
import jax.numpy as jnp
from jax import lax
from jax.experimental import pallas as pl
from jax.experimental.pallas import tpu as pltpu
from jax.sharding import Mesh
from jax.sharding import PartitionSpec as P

D = 4096
QH = 32
KVH = 4
HD = 128
GROUP = QH // KVH
FSDP = ("y", "x", "z")
OWNERS = ("y", "z")
REPLICA = ("yh", "c")
ALL = ("yh", "c", "y", "x", "z")

beta_one = 0.9
beta_two = 0.95
inner_rate = 0.05
decay_rate = 0.1
outer_rate = 0.7
outer_mu = 0.9

F32 = jnp.float32
BF16 = jnp.bfloat16
PARAMS = pltpu.CompilerParams(vmem_limit_bytes=48 << 20)


def shape_of(shape, dtype):
    return jax.ShapeDtypeStruct(shape, dtype)


def attention_body(q_ref, k_ref, t_ref, out_ref, p_ref):
    length = k_ref.shape[0]
    keys = k_ref[...]
    row = lax.broadcasted_iota(jnp.int32, (length, length), 0)
    col = lax.broadcasted_iota(jnp.int32, (length, length), 1)
    causal = row >= col
    for j in range(GROUP):
        head = q_ref[:, j * HD : (j + 1) * HD]
        scores = lax.dot_general(head, keys, (((1,), (1,)), ((), ())), preferred_element_type=F32)
        scores = jnp.where(causal, scores / math.sqrt(HD), -1e30)
        expd = jnp.exp(scores - jnp.max(scores, axis=-1, keepdims=True))
        attention = expd / jnp.sum(expd, axis=-1, keepdims=True)
        rows = slice(j * length, (j + 1) * length)
        p_ref[rows, :length] = attention.astype(BF16)
        p_ref[rows, length:] = t_ref[:, j * HD : (j + 1) * HD]
    both = p_ref[...]
    out_ref[0, 0] = lax.dot_general(
        both[:, :length], both, (((0,), (0,)), ((), ())), preferred_element_type=F32
    )


def attention_sums(queries, keys, targets):
    steps, length = queries.shape[:2]
    wide = GROUP * HD
    return pl.pallas_call(
        attention_body,
        grid=(steps, KVH),
        in_specs=[
            pl.BlockSpec((pl.Squeezed(), length, wide), lambda s, g: (s, 0, g)),
            pl.BlockSpec((pl.Squeezed(), length, HD), lambda s, g: (s, 0, g)),
            pl.BlockSpec((pl.Squeezed(), length, wide), lambda s, g: (s, 0, g)),
        ],
        out_specs=pl.BlockSpec((1, 1, length, length + HD), lambda s, g: (s, g, 0, 0)),
        out_shape=shape_of((steps, KVH, length, length + HD), F32),
        scratch_shapes=[pltpu.VMEM((GROUP * length, length + HD), BF16)],
        compiler_params=PARAMS,
        name="attention_sums",
    )(queries, keys, targets)


def slab_body(place_ref, *refs):
    half = len(refs) // 2
    for k in range(half):
        refs[half + k][...] = refs[k][...]


def slabs_of(place, layer_input, step, ys, xs):
    _, length, width = layer_input.shape
    wide = width // (ys * xs)

    def source(k):
        return pl.BlockSpec(
            (pl.Squeezed(), length, wide),
            lambda y, place: (step, 0, y * xs + lax.rem(place[0] + k, xs)),
        )

    return pl.pallas_call(
        slab_body,
        grid_spec=pltpu.PrefetchScalarGridSpec(
            num_scalar_prefetch=1,
            grid=(ys,),
            in_specs=[source(k) for k in range(xs)],
            out_specs=[pl.BlockSpec((length, wide), lambda y, place: (0, y))] * xs,
        ),
        out_shape=[shape_of((length, ys * wide), BF16)] * xs,
        compiler_params=PARAMS,
        name="slabs",
    )(place, *[layer_input] * xs)


def values_body(*refs):
    xs = len(refs) // 2
    weights = refs[xs][...]
    for k in range(xs):
        part = jnp.dot(refs[k][...], weights, preferred_element_type=F32)
        out = refs[xs + 1 + k]
        out[...] = (part * (1.0 / math.sqrt(D))).astype(out.dtype)


def partial_values(slabs, gathered):
    shape = (slabs[0].shape[0], gathered.shape[-1])
    return pl.pallas_call(
        values_body,
        out_shape=[shape_of(shape, F32)] + [shape_of(shape, BF16)] * (len(slabs) - 1),
        compiler_params=PARAMS,
        name="partial_values",
    )(*slabs, gathered)


def value_grad_body(*refs, tok_rep, step):
    parts, sums, out_ref = refs[:-2], refs[-2], refs[-1]
    length = out_ref.shape[0]
    total = parts[0][...]
    for part in parts[1:]:
        total = total + part[...].astype(F32)
    values = total.astype(BF16)
    for h in range(KVH):
        m = sums[h, :, :length]
        n = sums[h, :, length:]
        high = m.astype(BF16)
        low = (m - high.astype(F32)).astype(BF16)
        cols = slice(h * HD, (h + 1) * HD)
        part = values[:, cols]
        attended = jnp.dot(high, part, preferred_element_type=F32) + jnp.dot(
            low, part, preferred_element_type=F32
        )
        out_ref[:, cols] = ((attended - n) * (1.0 / tok_rep)).astype(BF16)


def value_gradient(parts, sums, step, tok_rep):
    whole = pl.BlockSpec(parts[0].shape, lambda i: (0, 0))
    return pl.pallas_call(
        lambda *refs: value_grad_body(*refs, tok_rep=tok_rep, step=step),
        grid=(1,),
        in_specs=[whole] * len(parts)
        + [pl.BlockSpec((pl.Squeezed(), *sums.shape[1:]), lambda i: (step, 0, 0, 0))],
        out_specs=whole,
        out_shape=shape_of(parts[0].shape, BF16),
        compiler_params=PARAMS,
        name="value_gradient",
    )(*parts, sums)


def gradient_body(*refs):
    half = len(refs) // 2
    inputs = jnp.concatenate([r[...] for r in refs[:half]], axis=0)
    stacked = jnp.concatenate([r[...] for r in refs[half:-1]], axis=0)
    total = lax.dot_general(inputs, stacked, (((0,), (0,)), ((), ())), preferred_element_type=F32)
    refs[-1][...] = (total * (1.0 / math.sqrt(D))).astype(BF16)


def partial_gradient(slabs, grads):
    shape = (slabs[0].shape[1], grads[0].shape[-1])
    return pl.pallas_call(
        gradient_body,
        out_shape=shape_of(shape, BF16),
        compiler_params=PARAMS,
        name="partial_gradient",
    )(*slabs, *grads)


def adam_body(*refs, step, floor, last):
    if step == 0:
        recv, theta_ref, m_out, u_out, theta_out, sent = refs
    else:
        recv, theta_ref, m_ref, u_ref, start_ref, m_out, u_out, theta_out, sent = refs
    gradient = recv[0].astype(F32)
    for z in range(1, recv.shape[0]):
        gradient = gradient + recv[z].astype(F32)
    moment_one = (1.0 - beta_one) * gradient
    moment_two = (1.0 - beta_two) * gradient * gradient
    if step > 0:
        moment_one = beta_one * m_ref[...] + moment_one
        moment_two = beta_two * u_ref[...] + moment_two
    corrected_one = moment_one / (1.0 - beta_one ** (step + 1))
    corrected_two = moment_two / (1.0 - beta_two ** (step + 1))
    theta = theta_ref[...]
    theta = theta - inner_rate * (
        corrected_one / (jnp.sqrt(corrected_two) + floor) + decay_rate * theta
    )
    m_out[...] = moment_one
    u_out[...] = moment_two
    theta_out[...] = theta
    if last:
        sent[...] = start_ref[...] - theta
    else:
        rounded = theta.astype(BF16)
        for z in range(recv.shape[0]):
            sent[z] = rounded


def adam(received, state, step, floor, last):
    shape = received.shape[1:]
    sent = shape_of(shape, F32) if last else shape_of(received.shape, BF16)
    return pl.pallas_call(
        lambda *refs: adam_body(*refs, step=step, floor=floor, last=last),
        out_shape=[shape_of(shape, F32)] * 3 + [sent],
        compiler_params=PARAMS,
        name="adam",
    )(received, *state)


def shifted(value, axis, k):
    size = lax.axis_size(axis)
    return lax.ppermute(value, axis, [(i, (i + k) % size) for i in range(size)])


def flipped(value, axis, mask):
    size = lax.axis_size(axis)
    return lax.ppermute(value, axis, [(i, i ^ mask) for i in range(size)])


def shards(layer_input, queries, keys, targets, value_weight, outer_momentum):
    inner_steps, length, _ = layer_input.shape
    shard_rows, columns = value_weight.shape
    ys, xs, zs = (lax.axis_size(a) for a in FSDP)
    owners = ys * zs
    tok_rep = length * owners * xs
    replicas = lax.axis_size(REPLICA)
    floor = math.sqrt(GROUP / (tok_rep * D))
    place = lax.axis_index("x").astype(jnp.int32).reshape(1)

    def routed(source, step):
        slabs = slabs_of(place, source, step, ys, xs)
        return [slabs[0]] + [shifted(slabs[k], "x", k) for k in range(1, xs)]

    rounded = value_weight.astype(BF16)
    gathered = lax.all_to_all(
        jnp.broadcast_to(rounded[None], (owners, shard_rows, columns)), OWNERS, 0, 0, tiled=True
    )
    slabs = routed(layer_input, 0)
    sums = attention_sums(queries, keys, targets)

    theta = value_weight
    state = ()
    for step in range(inner_steps):
        last = step == inner_steps - 1
        weights = gathered.reshape(owners * shard_rows, columns)
        parts = partial_values(slabs, weights)
        parts = [parts[0]] + [shifted(parts[k], "x", -k) for k in range(1, xs)]
        grad = value_gradient(parts, sums, step, tok_rep)
        grads = [grad] + [shifted(grad, "x", k) for k in range(1, xs)]
        scattered = partial_gradient(slabs, grads)
        scattered = scattered.reshape(owners, shard_rows, columns)
        if not last:
            scattered, source = lax.optimization_barrier((scattered, layer_input))
            slabs = routed(source, step + 1)
        received = lax.all_to_all(scattered, OWNERS, 0, 0, tiled=True)
        if not last:
            received, slabs = lax.optimization_barrier((received, slabs))
        args = (theta,) if step == 0 else (theta, *state, value_weight)
        m, u, theta, sent = adam(received, args, step, floor, last)
        state = (m, u)
        if not last:
            gathered = lax.all_to_all(sent, OWNERS, 0, 0, tiled=True)

    chip = sent + flipped(sent, "c", 1)
    mean_delta = (chip + flipped(chip, "yh", 1)) / replicas
    new_momentum = outer_mu * outer_momentum + mean_delta
    new_weight = value_weight - outer_rate * (mean_delta + outer_mu * new_momentum)
    return (new_weight, new_momentum)


def solution(mesh):
    split = Mesh(mesh.devices.reshape(2, 2, 2, 4, 8), ALL)
    tokens = P(None, REPLICA + FSDP, None)
    in_specs = (tokens, tokens, tokens, tokens, P(FSDP, None), P(FSDP, None))
    out_specs = (P(FSDP, None), P(FSDP, None))
    return jax.shard_map(
        shards, mesh=split, in_specs=in_specs, out_specs=out_specs, check_vma=False
    )
```

```python
import math

import jax
import jax.numpy as jnp
from jax import lax
from jax.experimental import pallas as pl
from jax.experimental.pallas import tpu as pltpu
from jax.sharding import Mesh
from jax.sharding import PartitionSpec as P

D = 4096
QH = 32
KVH = 4
HD = 128
GROUP = QH // KVH
FSDP = ("y", "x", "z")
REPLICA = ("yh", "c")
ALL = ("yh", "c", "y", "x", "z")

beta_one = 0.9
beta_two = 0.95
inner_rate = 0.05
decay_rate = 0.1
outer_rate = 0.7
outer_mu = 0.9

F32 = jnp.float32
BF16 = jnp.bfloat16
PARAMS = pltpu.CompilerParams(vmem_limit_bytes=12 << 20)


SMEM_SPEC = pl.BlockSpec(memory_space=pltpu.SMEM)
VMEM_SPEC = pl.BlockSpec(memory_space=pltpu.VMEM)
HBM_SPEC = pl.BlockSpec(memory_space=pltpu.HBM)
ANY_SPEC = pl.BlockSpec(memory_space=pl.ANY)


def without(body, at, count):
    return lambda *refs: body(*refs[:at], *refs[at + count :])


def shape_of(shape, dtype):
    return jax.ShapeDtypeStruct(shape, dtype)


def attention_body(
    place_ref, q_hbm, k_hbm, t_hbm, out_ref, q_ref, k_ref, t_ref, p_ref, sems, *, step
):
    heads, length, wide = q_ref.shape
    copies = []
    for g in range(heads):
        cols = pl.ds(g * wide, wide)
        near = pl.ds(g * HD, HD)
        copies.append(
            (
                pltpu.make_async_copy(q_hbm.at[step, :, cols], q_ref.at[g], sems.at[g, 0]),
                pltpu.make_async_copy(k_hbm.at[step, :, near], k_ref.at[g], sems.at[g, 1]),
                pltpu.make_async_copy(t_hbm.at[step, :, cols], t_ref.at[g], sems.at[g, 2]),
            )
        )
        for copy in copies[g]:
            copy.start()
    row = lax.broadcasted_iota(jnp.int32, (length, length), 0)
    col = lax.broadcasted_iota(jnp.int32, (length, length), 1)
    causal = row >= col
    shift = place_ref[0] * (heads // 2)
    for g in range(heads):
        for copy in copies[g]:
            copy.wait()
        keys = k_ref[g]
        for j in range(GROUP):
            head = q_ref[g, :, j * HD : (j + 1) * HD]
            scores = lax.dot_general(
                head, keys, (((1,), (1,)), ((), ())), preferred_element_type=F32
            )
            scores = jnp.where(causal, scores / math.sqrt(HD), -1e30)
            expd = jnp.exp(scores - jnp.max(scores, axis=-1, keepdims=True))
            attention = expd / jnp.sum(expd, axis=-1, keepdims=True)
            rows = slice(j * length, (j + 1) * length)
            p_ref[rows, :length] = attention.astype(BF16)
            p_ref[rows, length:] = t_ref[g, :, j * HD : (j + 1) * HD]
        both = p_ref[...]
        out_ref[lax.rem(g + shift, heads)] = lax.dot_general(
            both[:, :length], both, (((0,), (0,)), ((), ())), preferred_element_type=F32
        )


def attention_sums(place, queries, keys, targets, step, after):
    length = queries.shape[1]
    wide = GROUP * HD
    return pl.pallas_call(
        without(lambda *refs: attention_body(*refs, step=step), 4, len(after)),
        in_specs=[SMEM_SPEC] + [HBM_SPEC] * 3 + [ANY_SPEC] * len(after),
        out_shape=shape_of((KVH, length, length + HD), F32),
        scratch_shapes=[
            pltpu.VMEM((KVH, length, wide), BF16),
            pltpu.VMEM((KVH, length, HD), BF16),
            pltpu.VMEM((KVH, length, wide), BF16),
            pltpu.VMEM((GROUP * length, length + HD), BF16),
            pltpu.SemaphoreType.DMA((KVH, 3)),
        ],
        compiler_params=PARAMS,
        cost_estimate=pl.CostEstimate(flops=2 << 30, transcendentals=1 << 19, bytes_accessed=1 << 10),
        name="attention_sums",
    )(place, queries, keys, targets, *after)


def slab_body(place_ref, in_hbm, *refs, step, ys, xs, shifts):
    outs, sems = refs[:-1], refs[-1]
    wide = outs[0].shape[1] // ys
    copies = []
    for i, k in enumerate(shifts):
        for y in range(ys):
            start = pl.multiple_of((y * xs + lax.rem(place_ref[0] + k, xs)) * wide, wide)
            copies.append(
                pltpu.make_async_copy(
                    in_hbm.at[step, :, pl.ds(start, wide)],
                    outs[i].at[:, pl.ds(y * wide, wide)],
                    sems.at[i, y],
                )
            )
            copies[-1].start()
    for copy in copies:
        copy.wait()


def slabs_of(place, layer_input, step, ys, xs, shifts, after):
    _, length, width = layer_input.shape
    count = len(shifts)
    body = lambda *refs: slab_body(*refs, step=step, ys=ys, xs=xs, shifts=shifts)
    return list(
        pl.pallas_call(
            without(body, 2, len(after)),
            in_specs=[SMEM_SPEC, HBM_SPEC] + [ANY_SPEC] * len(after),
            out_specs=[HBM_SPEC] * count,
            out_shape=[shape_of((length, width // xs), BF16)] * count,
            scratch_shapes=[pltpu.SemaphoreType.DMA((count, ys))],
            compiler_params=PARAMS,
            cost_estimate=pl.CostEstimate(flops=1 << 30, transcendentals=0, bytes_accessed=1 << 10),
            name="slabs",
        )(place, layer_input, *after)
    )


def nothing_body(value_ref, after_ref, out_ref):
    pass


def passed_after(value, after):
    return pl.pallas_call(
        nothing_body,
        in_specs=[ANY_SPEC, ANY_SPEC],
        out_specs=ANY_SPEC,
        out_shape=shape_of(value.shape, value.dtype),
        input_output_aliases={0: 0},
        compiler_params=PARAMS,
        name="passed_after",
    )(value, after)


def values_body(*refs):
    x_refs, w_ref, out_refs = refs[:8], refs[8], refs[9:]
    zs, ys = w_ref.shape[:2]
    weights = jnp.concatenate([w_ref[z, y] for y in range(ys) for z in range(zs)], axis=0)
    for seq in range(2):
        for k in range(4):
            part = jnp.dot(x_refs[4 * seq + k][...], weights, preferred_element_type=F32)
            out = out_refs[k]
            out[seq] = (part * (1.0 / math.sqrt(D))).astype(out.dtype)


def partial_values(slabs, gathered):
    length = slabs[0].shape[0]
    columns = gathered.shape[-1]
    shape = (2, length, columns)
    return pl.pallas_call(
        values_body,
        out_shape=[shape_of(shape, F32)] + [shape_of(shape, BF16)] * 3,
        compiler_params=PARAMS,
        name="partial_values",
    )(*slabs, gathered)


def value_grad_body(v0, v1, v2, v3, own_ref, other_ref, out_ref, *, tok_rep):
    length = v0.shape[1]
    for seq, sums in enumerate((own_ref, other_ref)):
        total = (v0[seq] + v1[seq].astype(F32)) + (v2[seq].astype(F32) + v3[seq].astype(F32))
        values = total.astype(BF16)
        for h in range(sums.shape[0]):
            m = sums[h, :, :length]
            n = sums[h, :, length:]
            high = m.astype(BF16)
            low = (m - high.astype(F32)).astype(BF16)
            cols = slice(h * HD, (h + 1) * HD)
            part = values[:, cols]
            attended = jnp.dot(high, part, preferred_element_type=F32) + jnp.dot(
                low, part, preferred_element_type=F32
            )
            out_ref[seq, :, cols] = ((attended - n) * (1.0 / tok_rep)).astype(BF16)


def value_gradient(parts, own, other, tok_rep, after):
    return pl.pallas_call(
        without(lambda *refs: value_grad_body(*refs, tok_rep=tok_rep), 6, len(after)),
        in_specs=[VMEM_SPEC] * 6 + [ANY_SPEC] * len(after),
        out_shape=shape_of(parts[0].shape, BF16),
        compiler_params=PARAMS,
        name="value_gradient",
    )(*parts, own, other, *after)


def gradient_body(*refs):
    x_refs, g_refs, out_ref = refs[:8], refs[8:12], refs[12]
    zs, ys, rows = out_ref.shape[:3]
    inputs = jnp.concatenate([r[...] for r in x_refs], axis=0)
    grads = jnp.concatenate([g_refs[k][seq] for seq in range(2) for k in range(4)], axis=0)
    total = lax.dot_general(inputs, grads, (((0,), (0,)), ((), ())), preferred_element_type=F32)
    total = (total * (1.0 / math.sqrt(D))).astype(BF16)
    for y in range(ys):
        for z in range(zs):
            start = (y * zs + z) * rows
            out_ref[z, y] = total[start : start + rows]


def partial_gradient(slabs, grads, zs, ys):
    width = slabs[0].shape[1]
    columns = grads[0].shape[-1]
    return pl.pallas_call(
        gradient_body,
        out_shape=shape_of((zs, ys, width // (zs * ys), columns), BF16),
        compiler_params=PARAMS,
        name="partial_gradient",
    )(*slabs, *grads)


def adam_body(*refs, step, floor, last):
    if step == 0:
        recv, theta_ref, m_out, u_out, theta_out, sent = refs
    else:
        recv, theta_ref, m_ref, u_ref, start_ref, m_out, u_out, theta_out, sent = refs
    gradient = recv[0].astype(F32)
    for z in range(1, recv.shape[0]):
        gradient = gradient + recv[z].astype(F32)
    moment_one = (1.0 - beta_one) * gradient
    moment_two = (1.0 - beta_two) * gradient * gradient
    if step > 0:
        moment_one = beta_one * m_ref[...] + moment_one
        moment_two = beta_two * u_ref[...] + moment_two
    corrected_one = moment_one / (1.0 - beta_one ** (step + 1))
    corrected_two = moment_two / (1.0 - beta_two ** (step + 1))
    theta = theta_ref[...]
    theta = theta - inner_rate * (
        corrected_one / (jnp.sqrt(corrected_two) + floor) + decay_rate * theta
    )
    m_out[...] = moment_one
    u_out[...] = moment_two
    theta_out[...] = theta
    if last:
        sent[...] = start_ref[...] - theta
    else:
        rounded = theta.astype(BF16)
        for z in range(recv.shape[0]):
            sent[z] = rounded


def adam(received, state, step, floor, last, after):
    shape = received.shape[1:]
    sent = shape_of(shape, F32) if last else shape_of(received.shape, BF16)
    return pl.pallas_call(
        without(
            lambda *refs: adam_body(*refs, step=step, floor=floor, last=last),
            1 + len(state),
            len(after),
        ),
        in_specs=[VMEM_SPEC] * (1 + len(state)) + [ANY_SPEC] * len(after),
        out_shape=[shape_of(shape, F32)] * 3 + [sent],
        compiler_params=PARAMS,
        name="adam",
    )(received, *state, *after)


def shifted(value, axis, k):
    size = lax.axis_size(axis)
    return lax.ppermute(value, axis, [(i, (i + k) % size) for i in range(size)])


def flipped(value, axis, mask):
    size = lax.axis_size(axis)
    return lax.ppermute(value, axis, [(i, i ^ mask) for i in range(size)])


def pick(value, index, size, axis):
    return lax.dynamic_slice_in_dim(value, index * size, size, axis)


def shards(layer_input, queries, keys, targets, value_weight, outer_momentum):
    inner_steps, length, width = layer_input.shape
    shard_rows, columns = value_weight.shape
    half = columns // 2
    ys, xs, zs = (lax.axis_size(a) for a in FSDP)
    tok_rep = length * ys * xs * zs
    replicas = lax.axis_size(REPLICA)
    floor = math.sqrt(GROUP / (tok_rep * D))
    core, y = lax.axis_index("c"), lax.axis_index("y")
    x_place = lax.axis_index("x").astype(jnp.int32).reshape(1)
    y_place = y.astype(jnp.int32).reshape(1)

    def swapped(slab, k):
        pairs = [
            ((a * 2 + b) * xs + i, (b * 2 + a) * xs + (i + k) % xs)
            for a in range(2)
            for b in range(2)
            for i in range(xs)
        ]
        return lax.ppermute(slab, ("c", "y", "x"), pairs)

    def both_cores(own):
        return own + [flipped(slab, "c", 1) for slab in own]

    def sums_of(sums):
        heads = KVH // 2
        pairs = [(a, b) for a in range(2) for b in range(2)]
        own = [(a * 2 + b, b * 2 + a) for a, b in pairs]
        other = [(a * 2 + b, (1 - b) * 2 + a) for a, b in pairs]
        return (
            lax.ppermute(sums[:heads], ("c", "y"), own),
            lax.ppermute(sums[heads:], ("c", "y"), other),
        )

    every = tuple(range(xs))
    raw = slabs_of(x_place, layer_input, 0, ys, xs, every, ())
    own_slabs = [swapped(slab, k) for k, slab in enumerate(raw)]
    own_half = pick(value_weight, core, half, 1)
    first = own_half.astype(BF16)
    gathered = lax.all_to_all(
        jnp.broadcast_to(first[None], (zs * ys, *first.shape)), ("z", "y"), 0, 0, tiled=True
    ).reshape(zs, ys, shard_rows, half)
    sums = attention_sums(y_place, queries, keys, targets, 0, raw[:1])
    own_slabs = [passed_after(slab, sums) for slab in own_slabs]
    sums = sums_of(sums)
    slabs = both_cores(own_slabs)
    far_half = flipped(own_half, "y", 1)
    start = jnp.where(y == 0, jnp.stack([own_half, far_half]), jnp.stack([far_half, own_half]))

    theta = start
    state = ()
    for step in range(inner_steps):
        last = step == inner_steps - 1
        parts = list(partial_values(slabs, gathered))
        after = []
        if not last:
            head = parts[:1]
            later = attention_sums(y_place, queries, keys, targets, step + 1, head)
            moved = slabs_of(x_place, layer_input, step + 1, ys, xs, every[:1], head)
            after = [later, *moved]
        parts = [parts[0]] + [shifted(parts[k], "x", -k) for k in range(1, xs)]
        grad = value_gradient(parts, *sums, tok_rep, after)
        grads = [grad] + [shifted(grad, "x", k) for k in range(1, xs)]
        scattered = partial_gradient(slabs, grads, zs, ys)
        after = []
        if not last:
            sums = sums_of(later)
            moved += slabs_of(x_place, layer_input, step + 1, ys, xs, every[1:], [scattered])
            moved = [swapped(slab, k) for k, slab in enumerate(moved)]
            after = [*sums, *moved[:2]]
        received = lax.all_to_all(scattered, "z", 0, 0, tiled=True)
        args = (theta,) if step == 0 else (theta, *state, start)
        m, u, theta, sent = adam(received, args, step, floor, last, after)
        state = (m, u)
        if not last:
            gathered = lax.all_to_all(sent, "z", 0, 0, tiled=True)
            slabs = both_cores(moved)

    near = lax.dynamic_index_in_dim(sent, y, 0, False)
    far = lax.dynamic_index_in_dim(sent, 1 - y, 0, False)
    total = (near + flipped(far, ("yh", "y"), 1)) + (
        flipped(near, ("yh", "y"), 2) + flipped(far, ("yh", "y"), 3)
    )
    mean_half = total / replicas
    mean_other = flipped(mean_half, "c", 1)
    mean_delta = jnp.where(
        core == 0,
        jnp.concatenate([mean_half, mean_other], axis=1),
        jnp.concatenate([mean_other, mean_half], axis=1),
    )
    new_momentum = outer_mu * outer_momentum + mean_delta
    new_weight = value_weight - outer_rate * (mean_delta + outer_mu * new_momentum)
    return (new_weight, new_momentum)


def solution(mesh):
    split = Mesh(mesh.devices.reshape(2, 2, 2, 4, 8), ALL)
    tokens = P(None, REPLICA + FSDP, None)
    in_specs = (tokens, tokens, tokens, tokens, P(FSDP, None), P(FSDP, None))
    out_specs = (P(FSDP, None), P(FSDP, None))
    return jax.shard_map(
        shards, mesh=split, in_specs=in_specs, out_specs=out_specs, check_vma=False
    )
```

```python
import math

import jax
import jax.numpy as jnp
from jax import lax
from jax.experimental import pallas as pl
from jax.experimental.pallas import tpu as pltpu
from jax.sharding import Mesh
from jax.sharding import PartitionSpec as P

D = 4096
QH = 32
KVH = 4
HD = 128
GROUP = QH // KVH
FSDP = ("y", "x", "z")
REPLICA = ("yh", "c")
ALL = ("yh", "c", "y", "x", "z")

beta_one = 0.9
beta_two = 0.95
inner_rate = 0.05
decay_rate = 0.1
outer_rate = 0.7
outer_mu = 0.9

F32 = jnp.float32
BF16 = jnp.bfloat16
PARAMS = pltpu.CompilerParams(vmem_limit_bytes=12 << 20)


SMEM_SPEC = pl.BlockSpec(memory_space=pltpu.SMEM)
VMEM_SPEC = pl.BlockSpec(memory_space=pltpu.VMEM)
HBM_SPEC = pl.BlockSpec(memory_space=pltpu.HBM)
ANY_SPEC = pl.BlockSpec(memory_space=pl.ANY)


def without(body, at, count):
    return lambda *refs: body(*refs[:at], *refs[at + count :])


def shape_of(shape, dtype):
    return jax.ShapeDtypeStruct(shape, dtype)


def attention_body(
    place_ref, q_hbm, k_hbm, t_hbm, out_ref, q_ref, k_ref, t_ref, p_ref, sems, *, step
):
    heads, length, wide = q_ref.shape
    copies = []
    for g in range(heads):
        cols = pl.ds(g * wide, wide)
        near = pl.ds(g * HD, HD)
        copies.append(
            (
                pltpu.make_async_copy(q_hbm.at[step, :, cols], q_ref.at[g], sems.at[g, 0]),
                pltpu.make_async_copy(k_hbm.at[step, :, near], k_ref.at[g], sems.at[g, 1]),
                pltpu.make_async_copy(t_hbm.at[step, :, cols], t_ref.at[g], sems.at[g, 2]),
            )
        )
        for copy in copies[g]:
            copy.start()
    row = lax.broadcasted_iota(jnp.int32, (length, length), 0)
    col = lax.broadcasted_iota(jnp.int32, (length, length), 1)
    causal = row >= col
    shift = place_ref[0] * (heads // 2)
    for g in range(heads):
        for copy in copies[g]:
            copy.wait()
        keys = k_ref[g]
        for j in range(GROUP):
            head = q_ref[g, :, j * HD : (j + 1) * HD]
            scores = lax.dot_general(
                head, keys, (((1,), (1,)), ((), ())), preferred_element_type=F32
            )
            scores = jnp.where(causal, scores / math.sqrt(HD), -1e30)
            expd = jnp.exp(scores - jnp.max(scores, axis=-1, keepdims=True))
            attention = expd / jnp.sum(expd, axis=-1, keepdims=True)
            rows = slice(j * length, (j + 1) * length)
            p_ref[rows, :length] = attention.astype(BF16)
            p_ref[rows, length:] = t_ref[g, :, j * HD : (j + 1) * HD]
        both = p_ref[...]
        out_ref[lax.rem(g + shift, heads)] = lax.dot_general(
            both[:, :length], both, (((0,), (0,)), ((), ())), preferred_element_type=F32
        )


def attention_sums(place, queries, keys, targets, step, after):
    length = queries.shape[1]
    wide = GROUP * HD
    return pl.pallas_call(
        without(lambda *refs: attention_body(*refs, step=step), 4, len(after)),
        in_specs=[SMEM_SPEC] + [HBM_SPEC] * 3 + [ANY_SPEC] * len(after),
        out_shape=shape_of((KVH, length, length + HD), F32),
        scratch_shapes=[
            pltpu.VMEM((KVH, length, wide), BF16),
            pltpu.VMEM((KVH, length, HD), BF16),
            pltpu.VMEM((KVH, length, wide), BF16),
            pltpu.VMEM((GROUP * length, length + HD), BF16),
            pltpu.SemaphoreType.DMA((KVH, 3)),
        ],
        compiler_params=PARAMS,
        cost_estimate=pl.CostEstimate(flops=2 << 30, transcendentals=1 << 19, bytes_accessed=1 << 10),
        name="attention_sums",
    )(place, queries, keys, targets, *after)


def slab_body(place_ref, in_hbm, *refs, step, ys, xs, shifts):
    outs, sems = refs[:-1], refs[-1]
    wide = outs[0].shape[1] // ys
    copies = []
    for i, k in enumerate(shifts):
        for y in range(ys):
            start = pl.multiple_of((y * xs + lax.rem(place_ref[0] + k, xs)) * wide, wide)
            copies.append(
                pltpu.make_async_copy(
                    in_hbm.at[step, :, pl.ds(start, wide)],
                    outs[i].at[:, pl.ds(y * wide, wide)],
                    sems.at[i, y],
                )
            )
            copies[-1].start()
    for copy in copies:
        copy.wait()


def slabs_of(place, layer_input, step, ys, xs, shifts, after):
    _, length, width = layer_input.shape
    count = len(shifts)
    body = lambda *refs: slab_body(*refs, step=step, ys=ys, xs=xs, shifts=shifts)
    return list(
        pl.pallas_call(
            without(body, 2, len(after)),
            in_specs=[SMEM_SPEC, HBM_SPEC] + [ANY_SPEC] * len(after),
            out_specs=[HBM_SPEC] * count,
            out_shape=[shape_of((length, width // xs), BF16)] * count,
            scratch_shapes=[pltpu.SemaphoreType.DMA((count, ys))],
            compiler_params=PARAMS,
            cost_estimate=pl.CostEstimate(flops=1 << 30, transcendentals=0, bytes_accessed=1 << 10),
            name="slabs",
        )(place, layer_input, *after)
    )


def nothing_body(value_ref, after_ref, out_ref):
    pass


def passed_after(value, after):
    return pl.pallas_call(
        nothing_body,
        in_specs=[ANY_SPEC, ANY_SPEC],
        out_specs=ANY_SPEC,
        out_shape=shape_of(value.shape, value.dtype),
        input_output_aliases={0: 0},
        compiler_params=PARAMS,
        name="passed_after",
    )(value, after)


def values_body(*refs):
    x_refs, w_ref, out_refs = refs[:8], refs[8], refs[9:]
    zs, ys = w_ref.shape[:2]
    weights = jnp.concatenate([w_ref[z, y] for y in range(ys) for z in range(zs)], axis=0)
    for seq in range(2):
        for k in range(4):
            part = jnp.dot(x_refs[4 * seq + k][...], weights, preferred_element_type=F32)
            out = out_refs[k]
            out[seq] = (part * (1.0 / math.sqrt(D))).astype(out.dtype)


def partial_values(slabs, gathered):
    length = slabs[0].shape[0]
    columns = gathered.shape[-1]
    shape = (2, length, columns)
    return pl.pallas_call(
        values_body,
        out_shape=[shape_of(shape, F32)] + [shape_of(shape, BF16)] * 3,
        compiler_params=PARAMS,
        name="partial_values",
    )(*slabs, gathered)


def value_grad_body(v0, v1, v2, v3, own_ref, other_ref, out_ref, *, tok_rep):
    length = v0.shape[1]
    for seq, sums in enumerate((own_ref, other_ref)):
        total = (v0[seq] + v1[seq].astype(F32)) + (v2[seq].astype(F32) + v3[seq].astype(F32))
        values = total.astype(BF16)
        for h in range(sums.shape[0]):
            m = sums[h, :, :length]
            n = sums[h, :, length:]
            high = m.astype(BF16)
            low = (m - high.astype(F32)).astype(BF16)
            cols = slice(h * HD, (h + 1) * HD)
            part = values[:, cols]
            attended = jnp.dot(high, part, preferred_element_type=F32) + jnp.dot(
                low, part, preferred_element_type=F32
            )
            out_ref[seq, :, cols] = ((attended - n) * (1.0 / tok_rep)).astype(BF16)


def value_gradient(parts, own, other, tok_rep, after):
    return pl.pallas_call(
        without(lambda *refs: value_grad_body(*refs, tok_rep=tok_rep), 6, len(after)),
        in_specs=[VMEM_SPEC] * 6 + [ANY_SPEC] * len(after),
        out_shape=shape_of(parts[0].shape, BF16),
        compiler_params=PARAMS,
        name="value_gradient",
    )(*parts, own, other, *after)


def gradient_body(*refs):
    x_refs, g_refs, out_ref = refs[:8], refs[8:12], refs[12]
    zs, ys, rows = out_ref.shape[:3]
    inputs = jnp.concatenate([r[...] for r in x_refs], axis=0)
    grads = jnp.concatenate([g_refs[k][seq] for seq in range(2) for k in range(4)], axis=0)
    total = lax.dot_general(inputs, grads, (((0,), (0,)), ((), ())), preferred_element_type=F32)
    total = (total * (1.0 / math.sqrt(D))).astype(BF16)
    for y in range(ys):
        for z in range(zs):
            start = (y * zs + z) * rows
            out_ref[z, y] = total[start : start + rows]


def partial_gradient(slabs, grads, zs, ys):
    width = slabs[0].shape[1]
    columns = grads[0].shape[-1]
    return pl.pallas_call(
        gradient_body,
        out_shape=shape_of((zs, ys, width // (zs * ys), columns), BF16),
        compiler_params=PARAMS,
        name="partial_gradient",
    )(*slabs, *grads)


def adam_body(*refs, step, floor, last):
    if last:
        recv, theta_ref, m_ref, u_ref, start_ref, place_ref, near, far = refs
    elif step == 0:
        recv, theta_ref, m_out, u_out, theta_out, sent = refs
    else:
        recv, theta_ref, m_ref, u_ref, m_out, u_out, theta_out, sent = refs
    gradient = recv[0].astype(F32)
    for z in range(1, recv.shape[0]):
        gradient = gradient + recv[z].astype(F32)
    moment_one = (1.0 - beta_one) * gradient
    moment_two = (1.0 - beta_two) * gradient * gradient
    if step > 0:
        moment_one = beta_one * m_ref[...] + moment_one
        moment_two = beta_two * u_ref[...] + moment_two
    corrected_one = moment_one / (1.0 - beta_one ** (step + 1))
    corrected_two = moment_two / (1.0 - beta_two ** (step + 1))
    theta = theta_ref[...]
    theta = theta - inner_rate * (
        corrected_one / (jnp.sqrt(corrected_two) + floor) + decay_rate * theta
    )
    if last:
        delta = start_ref[...] - theta
        swap = place_ref[0] == 1
        near[...] = jnp.where(swap, delta[1], delta[0])
        far[...] = jnp.where(swap, delta[0], delta[1])
        return
    m_out[...] = moment_one
    u_out[...] = moment_two
    theta_out[...] = theta
    rounded = theta.astype(BF16)
    for z in range(recv.shape[0]):
        sent[z] = rounded


def adam(received, state, step, floor, last, after):
    shape = received.shape[1:]
    specs = [VMEM_SPEC] * (1 + len(state))
    outs = [shape_of(shape, F32)] * 3 + [shape_of(received.shape, BF16)]
    if last:
        specs[-1] = SMEM_SPEC
        outs = [shape_of(shape[1:], F32)] * 2
    return pl.pallas_call(
        without(
            lambda *refs: adam_body(*refs, step=step, floor=floor, last=last),
            1 + len(state),
            len(after),
        ),
        in_specs=specs + [ANY_SPEC] * len(after),
        out_shape=outs,
        compiler_params=PARAMS,
        name="adam",
    )(received, *state, *after)


def shifted(value, axis, k):
    size = lax.axis_size(axis)
    return lax.ppermute(value, axis, [(i, (i + k) % size) for i in range(size)])


def flipped(value, axis, mask):
    size = lax.axis_size(axis)
    return lax.ppermute(value, axis, [(i, i ^ mask) for i in range(size)])


def pick(value, index, size, axis):
    return lax.dynamic_slice_in_dim(value, index * size, size, axis)


def shards(layer_input, queries, keys, targets, value_weight, outer_momentum):
    inner_steps, length, width = layer_input.shape
    shard_rows, columns = value_weight.shape
    half = columns // 2
    ys, xs, zs = (lax.axis_size(a) for a in FSDP)
    tok_rep = length * ys * xs * zs
    replicas = lax.axis_size(REPLICA)
    floor = math.sqrt(GROUP / (tok_rep * D))
    core, y = lax.axis_index("c"), lax.axis_index("y")
    x_place = lax.axis_index("x").astype(jnp.int32).reshape(1)
    y_place = y.astype(jnp.int32).reshape(1)

    def swapped(slab, k):
        pairs = [
            ((a * 2 + b) * xs + i, (b * 2 + a) * xs + (i + k) % xs)
            for a in range(2)
            for b in range(2)
            for i in range(xs)
        ]
        return lax.ppermute(slab, ("c", "y", "x"), pairs)

    def both_cores(own):
        return own + [flipped(slab, "c", 1) for slab in own]

    def sums_of(sums):
        heads = KVH // 2
        pairs = [(a, b) for a in range(2) for b in range(2)]
        own = [(a * 2 + b, b * 2 + a) for a, b in pairs]
        other = [(a * 2 + b, (1 - b) * 2 + a) for a, b in pairs]
        return (
            lax.ppermute(sums[:heads], ("c", "y"), own),
            lax.ppermute(sums[heads:], ("c", "y"), other),
        )

    every = tuple(range(xs))
    raw = slabs_of(x_place, layer_input, 0, ys, xs, every, ())
    own_slabs = [swapped(slab, k) for k, slab in enumerate(raw)]
    own_half = pick(value_weight, core, half, 1)
    first = own_half.astype(BF16)
    gathered = lax.all_to_all(
        jnp.broadcast_to(first[None], (zs * ys, *first.shape)), ("z", "y"), 0, 0, tiled=True
    ).reshape(zs, ys, shard_rows, half)
    sums = attention_sums(y_place, queries, keys, targets, 0, raw[:1])
    own_slabs = [passed_after(slab, sums) for slab in own_slabs]
    sums = sums_of(sums)
    slabs = both_cores(own_slabs)
    far_half = flipped(own_half, "y", 1)
    start = jnp.where(y == 0, jnp.stack([own_half, far_half]), jnp.stack([far_half, own_half]))

    theta = start
    state = ()
    for step in range(inner_steps):
        last = step == inner_steps - 1
        parts = list(partial_values(slabs, gathered))
        after = []
        if not last:
            head = parts[:1]
            later = attention_sums(y_place, queries, keys, targets, step + 1, head)
            moved = slabs_of(x_place, layer_input, step + 1, ys, xs, every[:1], head)
            after = [later, *moved]
        parts = [parts[0]] + [shifted(parts[k], "x", -k) for k in range(1, xs)]
        grad = value_gradient(parts, *sums, tok_rep, after)
        grads = [grad] + [shifted(grad, "x", k) for k in range(1, xs)]
        scattered = partial_gradient(slabs, grads, zs, ys)
        after = []
        if not last:
            sums = sums_of(later)
            moved += slabs_of(x_place, layer_input, step + 1, ys, xs, every[1:], [scattered])
            moved = [swapped(slab, k) for k, slab in enumerate(moved)]
            after = [*sums, *moved[:2]]
        received = lax.all_to_all(scattered, "z", 0, 0, tiled=True)
        if last:
            args = (theta, *state, start, y_place)
            near, far = adam(received, args, step, floor, last, after)
        else:
            m, u, theta, sent = adam(received, (theta, *state), step, floor, last, after)
            state = (m, u)
            gathered = lax.all_to_all(sent, "z", 0, 0, tiled=True)
            slabs = both_cores(moved)

    total = (near + flipped(far, ("yh", "y"), 1)) + (
        flipped(near, ("yh", "y"), 2) + flipped(far, ("yh", "y"), 3)
    )
    mean_half = total / replicas
    mean_other = flipped(mean_half, "c", 1)
    mean_delta = jnp.where(
        core == 0,
        jnp.concatenate([mean_half, mean_other], axis=1),
        jnp.concatenate([mean_other, mean_half], axis=1),
    )
    new_momentum = outer_mu * outer_momentum + mean_delta
    new_weight = value_weight - outer_rate * (mean_delta + outer_mu * new_momentum)
    return (new_weight, new_momentum)


def solution(mesh):
    split = Mesh(mesh.devices.reshape(2, 2, 2, 4, 8), ALL)
    tokens = P(None, REPLICA + FSDP, None)
    in_specs = (tokens, tokens, tokens, tokens, P(FSDP, None), P(FSDP, None))
    out_specs = (P(FSDP, None), P(FSDP, None))
    return jax.shard_map(
        shards, mesh=split, in_specs=in_specs, out_specs=out_specs, check_vma=False
    )
```

```python
import math

import jax
import jax.numpy as jnp
from jax import lax
from jax.experimental import pallas as pl
from jax.experimental.pallas import tpu as pltpu
from jax.sharding import Mesh
from jax.sharding import PartitionSpec as P

D = 4096
QH = 32
KVH = 4
HD = 128
GROUP = QH // KVH
FSDP = ("y", "x", "z")
REPLICA = ("yh", "c")
ALL = ("yh", "c", "y", "x", "z")

beta_one = 0.9
beta_two = 0.95
inner_rate = 0.05
decay_rate = 0.1
outer_rate = 0.7
outer_mu = 0.9

F32 = jnp.float32
BF16 = jnp.bfloat16
PARAMS = pltpu.CompilerParams(vmem_limit_bytes=12 << 20)


SMEM_SPEC = pl.BlockSpec(memory_space=pltpu.SMEM)
VMEM_SPEC = pl.BlockSpec(memory_space=pltpu.VMEM)
HBM_SPEC = pl.BlockSpec(memory_space=pltpu.HBM)
ANY_SPEC = pl.BlockSpec(memory_space=pl.ANY)


def without(body, at, count):
    return lambda *refs: body(*refs[:at], *refs[at + count :])


def shape_of(shape, dtype):
    return jax.ShapeDtypeStruct(shape, dtype)


def attention_body(
    place_ref, q_hbm, k_hbm, t_hbm, out_ref, q_ref, k_ref, t_ref, p_ref, sems, *, step
):
    heads, length, wide = q_ref.shape
    copies = []
    for g in range(heads):
        cols = pl.ds(g * wide, wide)
        near = pl.ds(g * HD, HD)
        copies.append(
            (
                pltpu.make_async_copy(q_hbm.at[step, :, cols], q_ref.at[g], sems.at[g, 0]),
                pltpu.make_async_copy(k_hbm.at[step, :, near], k_ref.at[g], sems.at[g, 1]),
                pltpu.make_async_copy(t_hbm.at[step, :, cols], t_ref.at[g], sems.at[g, 2]),
            )
        )
        for copy in copies[g]:
            copy.start()
    row = lax.broadcasted_iota(jnp.int32, (length, length), 0)
    col = lax.broadcasted_iota(jnp.int32, (length, length), 1)
    causal = row >= col
    shift = place_ref[0] * (heads // 2)
    for g in range(heads):
        for copy in copies[g]:
            copy.wait()
        keys = k_ref[g]
        for j in range(GROUP):
            head = q_ref[g, :, j * HD : (j + 1) * HD]
            scores = lax.dot_general(
                head, keys, (((1,), (1,)), ((), ())), preferred_element_type=F32
            )
            scores = jnp.where(causal, scores / math.sqrt(HD), -1e30)
            expd = jnp.exp(scores - jnp.max(scores, axis=-1, keepdims=True))
            attention = expd / jnp.sum(expd, axis=-1, keepdims=True)
            rows = slice(j * length, (j + 1) * length)
            p_ref[rows, :length] = attention.astype(BF16)
            p_ref[rows, length:] = t_ref[g, :, j * HD : (j + 1) * HD]
        both = p_ref[...]
        out_ref[lax.rem(g + shift, heads)] = lax.dot_general(
            both[:, :length], both, (((0,), (0,)), ((), ())), preferred_element_type=F32
        )


def attention_sums(place, queries, keys, targets, step, after):
    length = queries.shape[1]
    wide = GROUP * HD
    return pl.pallas_call(
        without(lambda *refs: attention_body(*refs, step=step), 4, len(after)),
        in_specs=[SMEM_SPEC] + [HBM_SPEC] * 3 + [ANY_SPEC] * len(after),
        out_shape=shape_of((KVH, length, length + HD), F32),
        scratch_shapes=[
            pltpu.VMEM((KVH, length, wide), BF16),
            pltpu.VMEM((KVH, length, HD), BF16),
            pltpu.VMEM((KVH, length, wide), BF16),
            pltpu.VMEM((GROUP * length, length + HD), BF16),
            pltpu.SemaphoreType.DMA((KVH, 3)),
        ],
        compiler_params=PARAMS,
        cost_estimate=pl.CostEstimate(flops=2 << 30, transcendentals=1 << 19, bytes_accessed=1 << 10),
        name="attention_sums",
    )(place, queries, keys, targets, *after)


def slab_body(place_ref, in_hbm, *refs, step, ys, xs, shifts):
    outs, sems = refs[:-1], refs[-1]
    wide = outs[0].shape[1] // ys
    copies = []
    for i, k in enumerate(shifts):
        for y in range(ys):
            start = pl.multiple_of((y * xs + lax.rem(place_ref[0] + k, xs)) * wide, wide)
            copies.append(
                pltpu.make_async_copy(
                    in_hbm.at[step, :, pl.ds(start, wide)],
                    outs[i].at[:, pl.ds(y * wide, wide)],
                    sems.at[i, y],
                )
            )
            copies[-1].start()
    for copy in copies:
        copy.wait()


def slabs_of(place, layer_input, step, ys, xs, shifts, after):
    _, length, width = layer_input.shape
    count = len(shifts)
    body = lambda *refs: slab_body(*refs, step=step, ys=ys, xs=xs, shifts=shifts)
    return list(
        pl.pallas_call(
            without(body, 2, len(after)),
            in_specs=[SMEM_SPEC, HBM_SPEC] + [ANY_SPEC] * len(after),
            out_specs=[HBM_SPEC] * count,
            out_shape=[shape_of((length, width // xs), BF16)] * count,
            scratch_shapes=[pltpu.SemaphoreType.DMA((count, ys))],
            compiler_params=PARAMS,
            cost_estimate=pl.CostEstimate(flops=1 << 30, transcendentals=0, bytes_accessed=1 << 10),
            name="slabs",
        )(place, layer_input, *after)
    )


def nothing_body(value_ref, after_ref, out_ref):
    pass


def passed_after(value, after):
    return pl.pallas_call(
        nothing_body,
        in_specs=[ANY_SPEC, ANY_SPEC],
        out_specs=ANY_SPEC,
        out_shape=shape_of(value.shape, value.dtype),
        input_output_aliases={0: 0},
        compiler_params=PARAMS,
        name="passed_after",
    )(value, after)


def values_body(*refs):
    x_refs, w_ref, out_refs = refs[:8], refs[8], refs[9:]
    zs, ys = w_ref.shape[:2]
    weights = jnp.concatenate([w_ref[z, y] for y in range(ys) for z in range(zs)], axis=0)
    for seq in range(2):
        for k in range(4):
            part = jnp.dot(x_refs[4 * seq + k][...], weights, preferred_element_type=F32)
            out = out_refs[k]
            out[seq] = (part * (1.0 / math.sqrt(D))).astype(out.dtype)


def partial_values(slabs, gathered):
    length = slabs[0].shape[0]
    columns = gathered.shape[-1]
    shape = (2, length, columns)
    return pl.pallas_call(
        values_body,
        out_shape=[shape_of(shape, F32)] + [shape_of(shape, BF16)] * 3,
        compiler_params=PARAMS,
        name="partial_values",
    )(*slabs, gathered)


def value_grad_body(v0, v1, v2, v3, own_ref, other_ref, out_ref, *, tok_rep):
    length = v0.shape[1]
    for seq, sums in enumerate((own_ref, other_ref)):
        total = (v0[seq] + v1[seq].astype(F32)) + (v2[seq].astype(F32) + v3[seq].astype(F32))
        values = total.astype(BF16)
        for h in range(sums.shape[0]):
            m = sums[h, :, :length]
            n = sums[h, :, length:]
            high = m.astype(BF16)
            low = (m - high.astype(F32)).astype(BF16)
            cols = slice(h * HD, (h + 1) * HD)
            part = values[:, cols]
            attended = jnp.dot(high, part, preferred_element_type=F32) + jnp.dot(
                low, part, preferred_element_type=F32
            )
            out_ref[seq, :, cols] = ((attended - n) * (1.0 / tok_rep)).astype(BF16)


def value_gradient(parts, own, other, tok_rep, after):
    return pl.pallas_call(
        without(lambda *refs: value_grad_body(*refs, tok_rep=tok_rep), 6, len(after)),
        in_specs=[VMEM_SPEC] * 6 + [ANY_SPEC] * len(after),
        out_shape=shape_of(parts[0].shape, BF16),
        compiler_params=PARAMS,
        name="value_gradient",
    )(*parts, own, other, *after)


def gradient_body(*refs):
    x_refs, g_refs, out_ref = refs[:8], refs[8:12], refs[12]
    zs, ys, rows = out_ref.shape[:3]
    inputs = jnp.concatenate([r[...] for r in x_refs], axis=0)
    grads = jnp.concatenate([g_refs[k][seq] for seq in range(2) for k in range(4)], axis=0)
    total = lax.dot_general(inputs, grads, (((0,), (0,)), ((), ())), preferred_element_type=F32)
    total = (total * (1.0 / math.sqrt(D))).astype(BF16)
    for y in range(ys):
        for z in range(zs):
            start = (y * zs + z) * rows
            out_ref[z, y] = total[start : start + rows]


def partial_gradient(slabs, grads, zs, ys):
    width = slabs[0].shape[1]
    columns = grads[0].shape[-1]
    return pl.pallas_call(
        gradient_body,
        out_shape=shape_of((zs, ys, width // (zs * ys), columns), BF16),
        compiler_params=PARAMS,
        name="partial_gradient",
    )(*slabs, *grads)


def adam_body(*refs, step, floor, last):
    if last:
        recv, theta_ref, m_ref, u_ref, start_ref, place_ref, near, far = refs
    elif step == 0:
        recv, theta_ref, m_out, u_out, theta_out, sent = refs
    else:
        recv, theta_ref, m_ref, u_ref, m_out, u_out, theta_out, sent = refs
    gradient = recv[0].astype(F32)
    for z in range(1, recv.shape[0]):
        gradient = gradient + recv[z].astype(F32)
    moment_one = (1.0 - beta_one) * gradient
    moment_two = (1.0 - beta_two) * gradient * gradient
    if step > 0:
        moment_one = beta_one * m_ref[...] + moment_one
        moment_two = beta_two * u_ref[...] + moment_two
    corrected_one = moment_one / (1.0 - beta_one ** (step + 1))
    corrected_two = moment_two / (1.0 - beta_two ** (step + 1))
    theta = theta_ref[...]
    theta = theta - inner_rate * (
        corrected_one / (jnp.sqrt(corrected_two) + floor) + decay_rate * theta
    )
    if last:
        delta = start_ref[...] - theta
        swap = place_ref[0] == 1
        near[...] = jnp.where(swap, delta[1], delta[0])
        far[...] = jnp.where(swap, delta[0], delta[1])
        return
    m_out[...] = moment_one
    u_out[...] = moment_two
    theta_out[...] = theta
    rounded = theta.astype(BF16)
    for z in range(recv.shape[0]):
        sent[z] = rounded


def adam(received, state, step, floor, last, after):
    shape = received.shape[1:]
    specs = [VMEM_SPEC] * (1 + len(state))
    outs = [shape_of(shape, F32)] * 3 + [shape_of(received.shape, BF16)]
    if last:
        specs[-1] = SMEM_SPEC
        outs = [shape_of(shape[1:], F32)] * 2
    return pl.pallas_call(
        without(
            lambda *refs: adam_body(*refs, step=step, floor=floor, last=last),
            1 + len(state),
            len(after),
        ),
        in_specs=specs + [ANY_SPEC] * len(after),
        out_shape=outs,
        compiler_params=PARAMS,
        name="adam",
    )(received, *state, *after)


def shifted(value, axis, k):
    size = lax.axis_size(axis)
    return lax.ppermute(value, axis, [(i, (i + k) % size) for i in range(size)])


def flipped(value, axis, mask):
    size = lax.axis_size(axis)
    return lax.ppermute(value, axis, [(i, i ^ mask) for i in range(size)])


def pick(value, index, size, axis):
    return lax.dynamic_slice_in_dim(value, index * size, size, axis)


def shards(layer_input, queries, keys, targets, value_weight, outer_momentum):
    inner_steps, length, width = layer_input.shape
    shard_rows, columns = value_weight.shape
    half = columns // 2
    ys, xs, zs = (lax.axis_size(a) for a in FSDP)
    tok_rep = length * ys * xs * zs
    replicas = lax.axis_size(REPLICA)
    floor = math.sqrt(GROUP / (tok_rep * D))
    core, y = lax.axis_index("c"), lax.axis_index("y")
    x_place = lax.axis_index("x").astype(jnp.int32).reshape(1)
    y_place = y.astype(jnp.int32).reshape(1)

    def swapped(slab, k):
        pairs = [
            ((a * 2 + b) * xs + i, (b * 2 + a) * xs + (i + k) % xs)
            for a in range(2)
            for b in range(2)
            for i in range(xs)
        ]
        return lax.ppermute(slab, ("c", "y", "x"), pairs)

    def both_cores(own):
        return own + [flipped(slab, "c", 1) for slab in own]

    def sums_of(sums):
        heads = KVH // 2
        pairs = [(a, b) for a in range(2) for b in range(2)]
        own = [(a * 2 + b, b * 2 + a) for a, b in pairs]
        other = [(a * 2 + b, (1 - b) * 2 + a) for a, b in pairs]
        return (
            lax.ppermute(sums[:heads], ("c", "y"), own),
            lax.ppermute(sums[heads:], ("c", "y"), other),
        )

    every = tuple(range(xs))
    raw = slabs_of(x_place, layer_input, 0, ys, xs, every, ())
    own_slabs = [swapped(slab, k) for k, slab in enumerate(raw)]
    own_half = pick(value_weight, core, half, 1)
    first = own_half.astype(BF16)
    gathered = lax.all_to_all(
        jnp.broadcast_to(first[None], (zs * ys, *first.shape)), ("z", "y"), 0, 0, tiled=True
    ).reshape(zs, ys, shard_rows, half)
    sums = attention_sums(y_place, queries, keys, targets, 0, raw[:1])
    own_slabs = [passed_after(slab, sums) for slab in own_slabs]
    sums = sums_of(sums)
    slabs = both_cores(own_slabs)
    far_half = flipped(own_half, "y", 1)
    start = jnp.where(y == 0, jnp.stack([own_half, far_half]), jnp.stack([far_half, own_half]))

    theta = start
    state = ()
    for step in range(inner_steps):
        last = step == inner_steps - 1
        parts = list(partial_values(slabs, gathered))
        after = []
        if not last:
            head = parts[:1]
            later = attention_sums(y_place, queries, keys, targets, step + 1, head)
            moved = slabs_of(x_place, layer_input, step + 1, ys, xs, every[:1], head)
            after = [later, *moved]
        parts = [parts[0]] + [shifted(parts[k], "x", -k) for k in range(1, xs)]
        grad = value_gradient(parts, *sums, tok_rep, after)
        grads = [grad] + [shifted(grad, "x", k) for k in range(1, xs)]
        scattered = partial_gradient(slabs, grads, zs, ys)
        after = []
        if not last:
            sums = sums_of(later)
            moved += slabs_of(x_place, layer_input, step + 1, ys, xs, every[1:], [scattered])
            moved = [swapped(slab, k) for k, slab in enumerate(moved)]
            after = [*sums, moved[0]]
        received = lax.all_to_all(scattered, "z", 0, 0, tiled=True)
        if last:
            args = (theta, *state, start, y_place)
            near, far = adam(received, args, step, floor, last, after)
        else:
            m, u, theta, sent = adam(received, (theta, *state), step, floor, last, after)
            state = (m, u)
            gathered = lax.all_to_all(sent, "z", 0, 0, tiled=True)
            slabs = both_cores(moved)

    total = (near + flipped(far, ("yh", "y"), 1)) + (
        flipped(near, ("yh", "y"), 2) + flipped(far, ("yh", "y"), 3)
    )
    mean_half = total / replicas
    mean_other = flipped(mean_half, "c", 1)
    mean_delta = jnp.where(
        core == 0,
        jnp.concatenate([mean_half, mean_other], axis=1),
        jnp.concatenate([mean_other, mean_half], axis=1),
    )
    new_momentum = outer_mu * outer_momentum + mean_delta
    new_weight = value_weight - outer_rate * (mean_delta + outer_mu * new_momentum)
    return (new_weight, new_momentum)


def solution(mesh):
    split = Mesh(mesh.devices.reshape(2, 2, 2, 4, 8), ALL)
    tokens = P(None, REPLICA + FSDP, None)
    in_specs = (tokens, tokens, tokens, tokens, P(FSDP, None), P(FSDP, None))
    out_specs = (P(FSDP, None), P(FSDP, None))
    return jax.shard_map(
        shards, mesh=split, in_specs=in_specs, out_specs=out_specs, check_vma=False
    )
```
